32 devices in a mesh: req: 4 (over y, x), tp: 2 (over core), kv: 4 (over z).
Axes of the slice: x: 2, y: 2, z: 4, core: 2. Of those that a mesh axis runs over, the one named last changes fastest.
Arguments:
- hidden_in: bfloat16 [4, 512, 7168], P('req', 'tp', 'kv'), may hold values from -6 to 6
- lengths: int32 [4], P('req'), may hold values from 96 to 1536, as said below
- ln_gain: bfloat16 [7168], P('kv'), may hold values from 0.099609375 to 1.8984375
- ln_bias: bfloat16 [7168], P('kv'), may hold values from -3 to 3
- w_qkv: bfloat16 [7168, 768], P('kv', 'tp'), may hold values from -0.0625 to 0.0625
- qkv_bias: bfloat16 [768], P('tp'), may hold values from -3 to 3
- cache_keys: bfloat16 [4, 2, 1536, 128], P('req', 'tp', 'kv')
- cache_values: bfloat16 [4, 2, 1536, 128], P('req', 'tp', 'kv'), may hold values from -6 to 6
- w_out: bfloat16 [256, 7168], P('tp', 'kv'), may hold values from -0.375 to 0.375
- out_bias: bfloat16 [7168], P('kv'), may hold values from -3 to 3
Outputs:
- hidden_out: bfloat16 [4, 512, 7168], P('req', 'tp', 'kv')
- new_keys: bfloat16 [4, 2, 512, 128], P('req', 'tp', 'kv')
- new_values: bfloat16 [4, 2, 512, 128], P('req', 'tp', 'kv')
The draws below stay inside these ranges and needn't reach their ends.
Inputs may be any that keep to these rules, and one draw needn't show every extreme that they name: Request r's cache holds keys and values at its first lengths[r] positions; some request's cache is full in every draw.
All inputs are finite; a program needn't handle non-finite values.
Results may differ from the reference program's by a relative error of at most 0.012.
The reference program's roundings to bfloat16 on the way count: a program that leaves them out, or rounds other values in their place, can miss the bound.
Values may be sent and summed in bfloat16 or wider, within the bound.
A program may use at most 64 MiB of HBM per device.

```python
import jax
import jax.numpy as jnp
from jax import lax

D = 7168
HD = 128
HEADS = 2
GROUP = 512
MAXLEN = 1536
REQS = 4


def draw_lengths(key, part):
    first, second = jax.random.split(key)
    drawn = jax.random.randint(first, (REQS,), MAXLEN // 16, MAXLEN + 1, dtype=jnp.int32)
    chosen = jax.random.randint(second, (), 0, REQS, dtype=jnp.int32)
    return jnp.where(jnp.arange(REQS, dtype=jnp.int32) == chosen, MAXLEN, drawn).astype(jnp.int32)


def draw_cache_keys(key, part):
    shape = (REQS, HEADS, MAXLEN, HD)
    keys_drawn = jax.random.normal(key, shape, jnp.float32)
    return keys_drawn.astype(jnp.bfloat16)


def level_of(key, extent, cuts, low, high):
    def one(axis_at, shards_of):
        heights = jax.random.uniform(jax.random.fold_in(jax.random.fold_in(key, 6), axis_at), (shards_of,), jnp.float32, low / len(cuts), high / len(cuts))
        return jnp.repeat(jnp.exp(heights), extent[axis_at] // shards_of).reshape((-1,) + (1,) * (len(extent) - axis_at - 1))

    factor_of = one(*cuts[0])
    for cut in cuts[1:]:
        factor_of = factor_of * one(*cut)
    return factor_of


def bell_draw(key, extent, spread, most, cuts=(), kind=jnp.bfloat16):
    level = level_of(key, extent, cuts, -0.22, 0.18) if cuts else 1.0
    values = jax.random.normal(key, extent, jnp.float32) * spread * level
    return jnp.minimum(jnp.maximum(values, -most), most).astype(kind)


def setup_inputs(seed: int = 0) -> dict:
    key_of = jax.random.split(jax.random.key(seed), 11)
    return {
        "hidden_in": bell_draw(key_of[0], (REQS, GROUP, D), 1.0, 6.0, ((0, 4), (1, 2), (2, 4))),
        "lengths": draw_lengths(jax.random.fold_in(key_of[10], 71), 0),
        "ln_gain": jnp.clip(1.0 + 0.18 * jax.random.normal(key_of[2], (D,), jnp.float32), 0.099609375, 1.8984375).astype(jnp.bfloat16),
        "ln_bias": bell_draw(key_of[3], (D,), 0.5, 3.0, ((0, 4),)),
        "w_qkv": bell_draw(key_of[4], (D, 3 * HEADS * HD), D ** -0.5, 0.0625, ((0, 4), (1, 2))),
        "qkv_bias": bell_draw(key_of[5], (3 * HEADS * HD,), 0.5, 3.0, ((0, 2),)),
        "cache_keys": draw_cache_keys(jax.random.fold_in(key_of[10], 71), 0),
        "cache_values": bell_draw(key_of[7], (REQS, HEADS, MAXLEN, HD), 1.0, 6.0, ((0, 4), (1, 2), (2, 4))),
        "w_out": bell_draw(key_of[8], (HEADS * HD, D), (HEADS * HD) ** -0.5, 0.375, ((0, 2), (1, 4))),
        "out_bias": bell_draw(key_of[9], (D,), 0.5, 3.0, ((0, 4),)),
    }


epsilon = 1e-05
neg_large = -1e+30

def layer_norm(rows, gain, shift):
    values = rows.astype(jnp.float32)
    row_mean = lax.optimization_barrier(jnp.mean(values, axis=-1, keepdims=True))
    row_var = lax.optimization_barrier(jnp.mean(values * values, axis=-1, keepdims=True)) - row_mean * row_mean
    result = (values - row_mean) * lax.rsqrt(row_var + epsilon) * gain.astype(jnp.float32) + shift.astype(jnp.float32)
    return result.astype(jnp.bfloat16)

def attend_head(operands, length):
    queries, keys_new, values_new, keys_old, values_old = operands
    score_scale = HD ** (-0.5)
    old_scores = jnp.dot(queries, keys_old.T, preferred_element_type=jnp.float32) * score_scale
    new_scores = jnp.dot(queries, keys_new.T, preferred_element_type=jnp.float32) * score_scale
    old_seen = jnp.broadcast_to((jnp.arange(MAXLEN, dtype=jnp.int32) < length)[None, :], old_scores.shape)
    row_index = jnp.arange(GROUP, dtype=jnp.int32)
    new_seen = row_index[None, :] <= row_index[:, None]
    scores = jnp.concatenate([old_scores, new_scores], axis=1)
    seen = jnp.concatenate([old_seen, new_seen], axis=1)
    scores = jnp.where(seen, scores, neg_large)
    row_max = lax.optimization_barrier(jnp.max(scores, axis=1, keepdims=True))
    weights = jnp.where(seen, jnp.exp(scores - row_max), 0.0)
    row_sum = lax.optimization_barrier(jnp.sum(weights, axis=1, keepdims=True))
    all_values = jnp.concatenate([values_old, values_new], axis=0)
    mixed = jnp.dot(weights.astype(jnp.bfloat16), all_values, preferred_element_type=jnp.float32)
    return (mixed / row_sum).astype(jnp.bfloat16)

def reference(hidden_in, lengths, ln_gain, ln_bias, w_qkv, qkv_bias, cache_keys, cache_values, w_out, out_bias):
    normed_all = layer_norm(hidden_in, ln_gain, ln_bias)

    def one_request(operands):
        rows, normed, length, keys_old, values_old = operands
        projected = jnp.dot(normed, w_qkv, preferred_element_type=jnp.float32) + qkv_bias.astype(jnp.float32)
        projected = projected.astype(jnp.bfloat16).reshape(GROUP, HEADS, 3, HD).transpose(1, 2, 0, 3)
        queries = projected[:, 0]
        keys_new = projected[:, 1]
        values_new = projected[:, 2]
        heads_out = lax.map(lambda ops: attend_head(ops, length), (queries, keys_new, values_new, keys_old, values_old))
        joined = heads_out.transpose(1, 0, 2).reshape(GROUP, HEADS * HD)
        result = jnp.dot(joined, w_out, preferred_element_type=jnp.float32) + out_bias.astype(jnp.float32) + rows.astype(jnp.float32)
        return (result.astype(jnp.bfloat16), keys_new, values_new)
    hidden_out, new_keys, new_values = lax.map(one_request, (hidden_in, normed_all, lengths, cache_keys, cache_values))
    return (hidden_out, new_keys, new_values)
```

```python
import functools

import jax
import jax.numpy as jnp
from jax import lax
from jax.experimental import pallas as pl
from jax.experimental.pallas import tpu as pltpu
from jax.sharding import PartitionSpec as P

epsilon = 1e-05
neg_large = -1e30
MESH = pl.DeviceIdType.MESH
LANES = 128


def kernel(
    T, K, D,
    len_ref, x_hbm, w_hbm, keys_hbm, values_hbm, wout_hbm, params_ref, qkvb_ref,
    out_ref, nk_ref, nv_ref,
    x_v, w_v, k_v, v_v, wout_v,
    stat_out, stat_in, nrm, part, rbuf, q_buf, ot_out, ot_in, ml_out, ml_in, att_own, att_in,
    loc_sem, st_s, st_r, nm_s, nm_r, wo_s, wo_r, rs_s, rs_r, q_s, q_r, o_s, o_r, m_s, m_r, a_s, a_r,
):
    t = lax.axis_index("tp")
    z = lax.axis_index("kv")
    tok, feat = x_v.shape
    hd = k_v.shape[1]
    part_len = k_v.shape[0]
    group = T * tok
    qb = group // K
    c = min(tok, qb)
    tokp = stat_out.shape[1]

    def kv_peer(d):
        return lax.rem(z + d, K)

    def tp_peer(d):
        return lax.rem(t + d, T)

    barrier = pltpu.get_barrier_semaphore()
    for a in range(T):
        for b in range(K):
            if a or b:
                pl.semaphore_signal(barrier, inc=1, device_id={"tp": tp_peer(a), "kv": kv_peer(b)}, device_id_type=MESH)
    fetches = []
    for i, (src, dst) in enumerate(((x_hbm, x_v), (wout_hbm, wout_v.at[0]), (w_hbm, w_v), (keys_hbm, k_v), (values_hbm, v_v))):
        cp = pltpu.make_async_copy(src, dst, loc_sem.at[i])
        cp.start()
        fetches.append(cp)
    fetches[0].wait()

    rc = min(64, tok)
    p1s, p2s = [], []
    for r in range(tok // rc):
        p1 = jnp.zeros((rc, LANES), jnp.float32)
        p2 = jnp.zeros((rc, LANES), jnp.float32)
        for g in range(feat // LANES):
            xv = x_v[r * rc:(r + 1) * rc, g * LANES:(g + 1) * LANES].astype(jnp.float32)
            p1 = p1 + xv
            p2 = p2 + xv * xv
        p1s.append(p1)
        p2s.append(p2)
    if tok < tokp:
        p1s.append(jnp.zeros((tokp - tok, LANES), jnp.float32))
        p2s.append(jnp.zeros((tokp - tok, LANES), jnp.float32))
    s1 = jnp.sum(jnp.concatenate(p1s, axis=0).T, axis=0, keepdims=True)
    s2 = jnp.sum(jnp.concatenate(p2s, axis=0).T, axis=0, keepdims=True)
    stat_out[0:1, :] = s1
    stat_out[1:2, :] = s2
    stat_out[2:8, :] = jnp.zeros((6, tokp), jnp.float32)
    pl.semaphore_wait(barrier, T * K - 1)
    pending = []
    stat_copies = []
    for d in range(1, K):
        cp = pltpu.make_async_remote_copy(
            stat_out, stat_in.at[d - 1], st_s.at[d - 1], st_r.at[d - 1],
            device_id={"kv": kv_peer(d)}, device_id_type=MESH)
        cp.start()
        stat_copies.append(cp)
        pending.append(cp)
    fetches[1].wait()
    wo_copies = []
    for d in range(1, T):
        cp = pltpu.make_async_remote_copy(
            wout_v.at[0], wout_v.at[d], wo_s.at[d - 1], wo_r.at[d - 1],
            device_id={"tp": tp_peer(d)}, device_id_type=MESH)
        cp.start()
        wo_copies.append(cp)
        pending.append(cp)
    for cp in stat_copies:
        cp.wait_recv()
    for d in range(1, K):
        s1 = s1 + stat_in[d - 1, 0:1, :]
        s2 = s2 + stat_in[d - 1, 1:2, :]
    mean = s1 / D
    rstd = lax.rsqrt(s2 / D - mean * mean + epsilon)
    mean_c = jnp.broadcast_to(mean, (LANES, tokp)).T
    rstd_c = jnp.broadcast_to(rstd, (LANES, tokp)).T
    for r in range(tok // rc):
        mc = mean_c[r * rc:(r + 1) * rc]
        sc = rstd_c[r * rc:(r + 1) * rc]
        for g in range(feat // LANES):
            cols = slice(g * LANES, (g + 1) * LANES)
            xv = x_v[r * rc:(r + 1) * rc, cols].astype(jnp.float32)
            y = (xv - mc) * sc * params_ref[0:1, cols] + params_ref[1:2, cols]
            nrm[0, r * rc:(r + 1) * rc, cols] = y.astype(jnp.bfloat16)
    nm_copies = []
    for d in range(1, T):
        cp = pltpu.make_async_remote_copy(
            nrm.at[0], nrm.at[d], nm_s.at[d - 1], nm_r.at[d - 1],
            device_id={"tp": tp_peer(d)}, device_id_type=MESH)
        cp.start()
        nm_copies.append(cp)
        pending.append(cp)
    fetches[2].wait()

    rs_copies = []
    for d in range(T):
        if d:
            nm_copies[d - 1].wait_recv()
        part[d] = jnp.dot(nrm[d], w_v[...], preferred_element_type=jnp.float32)
        for i in range(tok // c):
            first = lax.rem(t - d + T, T) * tok + i * c
            owner = first // qb
            sub = lax.rem(first, qb) // c
            off = lax.rem(owner - z + K, K)
            slot = lax.rem(off + K - 1, K)
            cp = pltpu.make_async_remote_copy(
                part.at[d, pl.ds(i * c, c)], rbuf.at[slot, sub], rs_s.at[d * (tok // c) + i], rs_r.at[slot, sub],
                device_id={"kv": owner}, device_id_type=MESH)

            @pl.when(off != 0)
            def _():
                cp.start()

            @pl.when(off == 0)
            def _():
                rbuf[K - 1, sub] = part[d, i * c:(i + 1) * c]

            rs_copies.append((cp, off))
    fetches[3].wait()
    fetches[4].wait()
    vt_old = v_v[...].T
    for e in range(K - 1):
        for s in range(qb // c):
            pltpu.make_async_remote_copy(
                rbuf.at[e, s], rbuf.at[e, s], rs_s.at[0], rs_r.at[e, s],
                device_id={"kv": kv_peer(1)}, device_id_type=MESH).wait_recv()
    total = rbuf[K - 1]
    for e in range(K - 1):
        total = total + rbuf[e]
    proj = (total.reshape(qb, 3 * hd) + qkvb_ref[...]).astype(jnp.bfloat16)
    k_new = proj[:, hd:2 * hd]
    v_new = proj[:, 2 * hd:]
    q_buf[0] = proj[:, :hd]
    q_copies = []
    for d in range(1, K):
        cp = pltpu.make_async_remote_copy(
            q_buf.at[0], q_buf.at[d], q_s.at[d - 1], q_r.at[d - 1],
            device_id={"kv": kv_peer(d)}, device_id_type=MESH)
        cp.start()
        q_copies.append(cp)
        pending.append(cp)
    nk_ref[...] = k_new
    nv_ref[...] = v_new
    vt_new = v_new.T
    length = len_ref[0]
    scale = hd ** (-0.5)
    dims = (((1,), (1,)), ((), ()))
    old_seen = (z * part_len + lax.broadcasted_iota(jnp.int32, (part_len, qb), 0)) < length
    key_at = z * qb + lax.broadcasted_iota(jnp.int32, (qb, qb), 0)
    query_in = lax.broadcasted_iota(jnp.int32, (qb, qb), 1)

    def attend(d):
        q = q_buf[d]
        s_old = lax.dot_general(k_v[...], q, dims, preferred_element_type=jnp.float32) * scale
        s_new = lax.dot_general(k_new, q, dims, preferred_element_type=jnp.float32) * scale
        new_seen = key_at <= lax.rem(z - d + K, K) * qb + query_in
        s_old = jnp.where(old_seen, s_old, neg_large)
        s_new = jnp.where(new_seen, s_new, neg_large)
        m = jnp.maximum(jnp.max(s_old, axis=0, keepdims=True), jnp.max(s_new, axis=0, keepdims=True))
        w_old = jnp.where(old_seen, jnp.exp(s_old - m), 0.0)
        w_new = jnp.where(new_seen, jnp.exp(s_new - m), 0.0)
        l = jnp.sum(w_old, axis=0, keepdims=True) + jnp.sum(w_new, axis=0, keepdims=True)
        ot = jnp.dot(vt_old, w_old.astype(jnp.bfloat16), preferred_element_type=jnp.float32)
        ot = ot + jnp.dot(vt_new, w_new.astype(jnp.bfloat16), preferred_element_type=jnp.float32)
        return m, l, ot

    m0, l0, ot0 = attend(0)
    o_copies = []
    for d in range(1, K):
        q_copies[d - 1].wait_recv()
        m, l, ot = attend(d)
        ot_out[d - 1] = ot.astype(jnp.bfloat16)
        ml_out[d - 1, 0:1, :] = m
        ml_out[d - 1, 1:2, :] = l
        ml_out[d - 1, 2:8, :] = jnp.zeros((6, qb), jnp.float32)
        back = {"kv": kv_peer(K - d)}
        cpm = pltpu.make_async_remote_copy(
            ml_out.at[d - 1], ml_in.at[d - 1], m_s.at[d - 1], m_r.at[d - 1], device_id=back, device_id_type=MESH)
        cpm.start()
        cpo = pltpu.make_async_remote_copy(
            ot_out.at[d - 1], ot_in.at[d - 1], o_s.at[d - 1], o_r.at[d - 1], device_id=back, device_id_type=MESH)
        cpo.start()
        o_copies += [cpm, cpo]
        pending += [cpm, cpo]
    for cp in o_copies:
        cp.wait_recv()
    top = m0
    for d in range(1, K):
        top = jnp.maximum(top, ml_in[d - 1, 0:1, :])
    f = jnp.exp(m0 - top)
    l_all = l0 * f
    o_all = ot0 * f
    for d in range(1, K):
        f = jnp.exp(ml_in[d - 1, 0:1, :] - top)
        l_all = l_all + ml_in[d - 1, 1:2, :] * f
        o_all = o_all + ot_in[d - 1].astype(jnp.float32) * f
    att_own[...] = (o_all / l_all).T.astype(jnp.bfloat16)

    att_copies = []
    for s in range(qb // c):
        first = z * qb + s * c
        tp_own = first // tok
        slot = lax.rem(tp_own - t + T, T)
        at = lax.rem(first, tok) // c
        for e in list(range(1, K)) + [0]:
            cp = pltpu.make_async_remote_copy(
                att_own.at[pl.ds(s * c, c)], att_in.at[slot, at], a_s.at[s, e], a_r.at[slot, at],
                device_id={"tp": tp_own, "kv": kv_peer(e)}, device_id_type=MESH)
            if e:
                cp.start()
                att_copies.append((cp, None))
            else:
                @pl.when(slot != 0)
                def _():
                    cp.start()

                @pl.when(slot == 0)
                def _():
                    att_in[0, at] = att_own[s * c:(s + 1) * c]

                att_copies.append((cp, slot))
    for cp in wo_copies:
        cp.wait_recv()
    for d in range(T):
        for i in range(tok // c):
            def wait_in():
                pltpu.make_async_remote_copy(
                    att_in.at[d, i], att_in.at[d, i], a_s.at[0, 0], a_r.at[d, i],
                    device_id={"kv": kv_peer(1)}, device_id_type=MESH).wait_recv()
            if d:
                wait_in()
            else:
                pl.when((t * tok + i * c) // qb != z)(wait_in)
    att = jnp.concatenate([att_in[d].reshape(tok, hd) for d in range(T)], axis=1)
    wide = 256 if feat % 256 == 0 else feat
    for g in range(feat // wide):
        cols = slice(g * wide, (g + 1) * wide)
        w = jnp.concatenate([wout_v[d, :, cols] for d in range(T)], axis=0)
        y = jnp.dot(att, w, preferred_element_type=jnp.float32)
        y = y + params_ref[2:3, cols] + x_v[:, cols].astype(jnp.float32)
        out_ref[:, cols] = y.astype(jnp.bfloat16)

    for cp in pending:
        cp.wait_send()
    for cp, off in rs_copies:
        pl.when(off != 0)(cp.wait_send)
    for cp, slot in att_copies:
        if slot is None:
            cp.wait_send()
        else:
            pl.when(slot != 0)(cp.wait_send)


def on_device(T, K, hidden_in, lengths, ln_gain, ln_bias, w_qkv, qkv_bias, cache_keys, cache_values, w_out, out_bias):
    _, tok, feat = hidden_in.shape
    hd = cache_keys.shape[3]
    part_len = cache_keys.shape[2]
    group = T * tok
    qb = group // K
    c = min(tok, qb)
    tokp = max(tok, LANES)
    params = jnp.stack([ln_gain, ln_bias, out_bias]).astype(jnp.float32)
    qkvb = qkv_bias.astype(jnp.float32)[None]
    bf, f32 = jnp.bfloat16, jnp.float32
    dma = pltpu.SemaphoreType.DMA
    any_spec = pl.BlockSpec(memory_space=pl.ANY)
    vm = pl.BlockSpec(memory_space=pltpu.VMEM)
    n1 = max(T - 1, 1)
    out, nk, nv = pl.pallas_call(
        functools.partial(kernel, T, K, feat * K),
        out_shape=(
            jax.ShapeDtypeStruct((tok, feat), bf),
            jax.ShapeDtypeStruct((qb, hd), bf),
            jax.ShapeDtypeStruct((qb, hd), bf),
        ),
        in_specs=[pl.BlockSpec(memory_space=pltpu.SMEM)] + [any_spec] * 5 + [vm, vm],
        out_specs=(vm, vm, vm),
        scratch_shapes=[
            pltpu.VMEM((tok, feat), bf),
            pltpu.VMEM((feat, 3 * hd), bf),
            pltpu.VMEM((part_len, hd), bf),
            pltpu.VMEM((part_len, hd), bf),
            pltpu.VMEM((T, hd, feat), bf),
            pltpu.VMEM((8, tokp), f32),
            pltpu.VMEM((K - 1, 8, tokp), f32),
            pltpu.VMEM((T, tok, feat), bf),
            pltpu.VMEM((T, tok, 3 * hd), f32),
            pltpu.VMEM((K, qb // c, c, 3 * hd), f32),
            pltpu.VMEM((K, qb, hd), bf),
            pltpu.VMEM((K - 1, hd, qb), bf),
            pltpu.VMEM((K - 1, hd, qb), bf),
            pltpu.VMEM((K - 1, 8, qb), f32),
            pltpu.VMEM((K - 1, 8, qb), f32),
            pltpu.VMEM((qb, hd), bf),
            pltpu.VMEM((T, tok // c, c, hd), bf),
            dma((5,)),
            dma((K - 1,)), dma((K - 1,)),
            dma((n1,)), dma((n1,)),
            dma((n1,)), dma((n1,)),
            dma((T * (tok // c),)), dma((K - 1, qb // c)),
            dma((K - 1,)), dma((K - 1,)),
            dma((K - 1,)), dma((K - 1,)),
            dma((K - 1,)), dma((K - 1,)),
            dma((qb // c, K)), dma((T, tok // c)),
        ],
        compiler_params=pltpu.CompilerParams(
            collective_id=0, has_side_effects=True, vmem_limit_bytes=48 * 1024 * 1024),
    )(lengths, hidden_in[0], w_qkv, cache_keys[0, 0], cache_values[0, 0], w_out, params, qkvb)
    return out[None], nk[None, None], nv[None, None]


def solution(mesh):
    placed = (
        P("req", "tp", "kv"),
        P("req"),
        P("kv"),
        P("kv"),
        P("kv", "tp"),
        P("tp"),
        P("req", "tp", "kv", None),
        P("req", "tp", "kv", None),
        P("tp", "kv"),
        P("kv"),
    )
    return jax.shard_map(
        functools.partial(on_device, mesh.shape["tp"], mesh.shape["kv"]),
        mesh=mesh,
        in_specs=placed,
        out_specs=(P("req", "tp", "kv"), P("req", "tp", "kv", None), P("req", "tp", "kv", None)),
        check_vma=False,
    )
```

```python
import functools

import jax
import jax.numpy as jnp
from jax import lax
from jax.experimental import pallas as pl
from jax.experimental.pallas import tpu as pltpu
from jax.sharding import PartitionSpec as P

epsilon = 1e-05
neg_large = -1e30
MESH = pl.DeviceIdType.MESH
LANES = 128


def kernel(
    T, K, D,
    len_ref, x_hbm, w_hbm, keys_hbm, values_hbm, wout_hbm, gain_ref, lnb_ref, outb_ref, qkvb_ref,
    out_ref, nk_ref, nv_ref,
    x_v, w_v, k_v, v_v, wout_v,
    stat_out, stat_in, nrm, part_q, part_kv, rbuf_q, rbuf_kv, q_buf, ot_out, ot_in, ml_out, ml_in, att_own, att_in,
    loc_sem, st_s, st_r, nm_s, nm_r, wo_s, wo_r, rq_s, rq_r, rkv_s, rkv_r, q_s, q_r, o_s, o_r, m_s, m_r, a_s, a_r,
):
    t = lax.axis_index("tp")
    z = lax.axis_index("kv")
    tok, feat = x_v.shape
    hd = k_v.shape[1]
    part_len = k_v.shape[0]
    group = T * tok
    qb = group // K
    c = min(tok, qb)
    tokp = stat_out.shape[1]

    def kv_peer(d):
        return lax.rem(z + d, K)

    def tp_peer(d):
        return lax.rem(t + d, T)

    def row(ref):
        return ref[...].astype(jnp.float32).reshape(1, ref.shape[0])

    barrier = pltpu.get_barrier_semaphore()
    for a in range(T):
        for b in range(K):
            if a or b:
                pl.semaphore_signal(barrier, inc=1, device_id={"tp": tp_peer(a), "kv": kv_peer(b)}, device_id_type=MESH)
    fetches = []
    for i, (src, dst) in enumerate(((x_hbm, x_v), (wout_hbm, wout_v.at[0]), (w_hbm, w_v), (keys_hbm, k_v), (values_hbm, v_v))):
        cp = pltpu.make_async_copy(src, dst, loc_sem.at[i])
        cp.start()
        fetches.append(cp)
    fetches[0].wait()

    rc = min(64, tok)
    p1s, p2s = [], []
    for r in range(tok // rc):
        p1 = jnp.zeros((rc, LANES), jnp.float32)
        p2 = jnp.zeros((rc, LANES), jnp.float32)
        for g in range(feat // LANES):
            xv = x_v[r * rc:(r + 1) * rc, g * LANES:(g + 1) * LANES].astype(jnp.float32)
            p1 = p1 + xv
            p2 = p2 + xv * xv
        p1s.append(p1)
        p2s.append(p2)
    if tok < tokp:
        p1s.append(jnp.zeros((tokp - tok, LANES), jnp.float32))
        p2s.append(jnp.zeros((tokp - tok, LANES), jnp.float32))
    s1 = jnp.sum(jnp.concatenate(p1s, axis=0).T, axis=0, keepdims=True)
    s2 = jnp.sum(jnp.concatenate(p2s, axis=0).T, axis=0, keepdims=True)
    stat_out[0:1, :] = s1
    stat_out[1:2, :] = s2
    stat_out[2:8, :] = jnp.zeros((6, tokp), jnp.float32)
    pl.semaphore_wait(barrier, T * K - 1)
    pending = []
    stat_copies = []
    for d in range(1, K):
        cp = pltpu.make_async_remote_copy(
            stat_out, stat_in.at[d - 1], st_s.at[d - 1], st_r.at[d - 1],
            device_id={"kv": kv_peer(d)}, device_id_type=MESH)
        cp.start()
        stat_copies.append(cp)
        pending.append(cp)
    fetches[1].wait()
    wo_copies = []
    for d in range(1, T):
        cp = pltpu.make_async_remote_copy(
            wout_v.at[0], wout_v.at[d], wo_s.at[d - 1], wo_r.at[d - 1],
            device_id={"tp": tp_peer(d)}, device_id_type=MESH)
        cp.start()
        wo_copies.append(cp)
        pending.append(cp)
    for cp in stat_copies:
        cp.wait_recv()
    for d in range(1, K):
        s1 = s1 + stat_in[d - 1, 0:1, :]
        s2 = s2 + stat_in[d - 1, 1:2, :]
    gain = row(gain_ref)
    shift = row(lnb_ref)
    mean = s1 / D
    rstd = lax.rsqrt(s2 / D - mean * mean + epsilon)
    mean_c = jnp.broadcast_to(mean, (LANES, tokp)).T
    rstd_c = jnp.broadcast_to(rstd, (LANES, tokp)).T
    for r in range(tok // rc):
        mc = mean_c[r * rc:(r + 1) * rc]
        sc = rstd_c[r * rc:(r + 1) * rc]
        for g in range(feat // LANES):
            cols = slice(g * LANES, (g + 1) * LANES)
            xv = x_v[r * rc:(r + 1) * rc, cols].astype(jnp.float32)
            y = (xv - mc) * sc * gain[:, cols] + shift[:, cols]
            nrm[0, r * rc:(r + 1) * rc, cols] = y.astype(jnp.bfloat16)
    nm_copies = []
    for d in range(1, T):
        cp = pltpu.make_async_remote_copy(
            nrm.at[0], nrm.at[d], nm_s.at[d - 1], nm_r.at[d - 1],
            device_id={"tp": tp_peer(d)}, device_id_type=MESH)
        cp.start()
        nm_copies.append(cp)
        pending.append(cp)
    fetches[2].wait()

    rs_copies = []

    def scatter(d, part, rbuf, s_sem, r_sem):
        for i in range(tok // c):
            first = lax.rem(t - d + T, T) * tok + i * c
            owner = first // qb
            sub = lax.rem(first, qb) // c
            off = lax.rem(owner - z + K, K)
            slot = lax.rem(off + K - 1, K)
            cp = pltpu.make_async_remote_copy(
                part.at[d, pl.ds(i * c, c)], rbuf.at[slot, sub], s_sem.at[d * (tok // c) + i], r_sem.at[slot, sub],
                device_id={"kv": owner}, device_id_type=MESH)

            @pl.when(off != 0)
            def _():
                cp.start()

            @pl.when(off == 0)
            def _():
                rbuf[K - 1, sub] = part[d, i * c:(i + 1) * c]

            rs_copies.append((cp, off))

    def gathered(rbuf, s_sem, r_sem, bias):
        for e in range(K - 1):
            for s in range(qb // c):
                pltpu.make_async_remote_copy(
                    rbuf.at[e, s], rbuf.at[e, s], s_sem.at[0], r_sem.at[e, s],
                    device_id={"kv": kv_peer(1)}, device_id_type=MESH).wait_recv()
        total = rbuf[K - 1]
        for e in range(K - 1):
            total = total + rbuf[e]
        return (total.reshape(qb, rbuf.shape[3]) + bias).astype(jnp.bfloat16)

    def project(d, lo, hi, part):
        part[d] = jnp.dot(nrm[d], w_v[:, lo:hi], preferred_element_type=jnp.float32)

    project(0, 0, hd, part_q)
    scatter(0, part_q, rbuf_q, rq_s, rq_r)
    project(0, hd, 3 * hd, part_kv)
    for d in range(1, T):
        nm_copies[d - 1].wait_recv()
        project(d, 0, hd, part_q)
        scatter(d, part_q, rbuf_q, rq_s, rq_r)
    scatter(0, part_kv, rbuf_kv, rkv_s, rkv_r)
    for d in range(1, T):
        project(d, hd, 3 * hd, part_kv)
        scatter(d, part_kv, rbuf_kv, rkv_s, rkv_r)
    fetches[3].wait()
    fetches[4].wait()
    vt_old = v_v[...].T
    qkv_bias = row(qkvb_ref)
    q_buf[0] = gathered(rbuf_q, rq_s, rq_r, qkv_bias[:, :hd])
    q_copies = []
    for d in range(1, K):
        cp = pltpu.make_async_remote_copy(
            q_buf.at[0], q_buf.at[d], q_s.at[d - 1], q_r.at[d - 1],
            device_id={"kv": kv_peer(d)}, device_id_type=MESH)
        cp.start()
        q_copies.append(cp)
        pending.append(cp)
    length = len_ref[0]
    scale = hd ** (-0.5)
    dims = (((1,), (1,)), ((), ()))
    old_seen = (z * part_len + lax.broadcasted_iota(jnp.int32, (part_len, qb), 0)) < length
    key_at = z * qb + lax.broadcasted_iota(jnp.int32, (qb, qb), 0)
    query_in = lax.broadcasted_iota(jnp.int32, (qb, qb), 1)

    def weigh(keys, q, seen, vt):
        s = lax.dot_general(keys, q, dims, preferred_element_type=jnp.float32) * scale
        s = jnp.where(seen, s, neg_large)
        m = jnp.max(s, axis=0, keepdims=True)
        w = jnp.where(seen, jnp.exp(s - m), 0.0)
        l = jnp.sum(w, axis=0, keepdims=True)
        return m, l, jnp.dot(vt, w.astype(jnp.bfloat16), preferred_element_type=jnp.float32)

    olds = []
    for d in range(K):
        if d:
            q_copies[d - 1].wait_recv()
        olds.append(weigh(k_v[...], q_buf[d], old_seen, vt_old))
    kv_new = gathered(rbuf_kv, rkv_s, rkv_r, qkv_bias[:, hd:])
    k_new = kv_new[:, :hd]
    v_new = kv_new[:, hd:]
    vt_new = v_new.T

    def attend(d):
        m_old, l_old, ot_old = olds[d]
        new_seen = key_at <= lax.rem(z - d + K, K) * qb + query_in
        m_new, l_new, ot_new = weigh(k_new, q_buf[d], new_seen, vt_new)
        m = jnp.maximum(m_old, m_new)
        f_old = jnp.exp(m_old - m)
        f_new = jnp.exp(m_new - m)
        return m, l_old * f_old + l_new * f_new, ot_old * f_old + ot_new * f_new

    o_copies = []
    for d in range(1, K):
        m, l, ot = attend(d)
        ot_out[d - 1] = ot.astype(jnp.bfloat16)
        ml_out[d - 1, 0:1, :] = m
        ml_out[d - 1, 1:2, :] = l
        ml_out[d - 1, 2:8, :] = jnp.zeros((6, qb), jnp.float32)
        back = {"kv": kv_peer(K - d)}
        cpm = pltpu.make_async_remote_copy(
            ml_out.at[d - 1], ml_in.at[d - 1], m_s.at[d - 1], m_r.at[d - 1], device_id=back, device_id_type=MESH)
        cpm.start()
        cpo = pltpu.make_async_remote_copy(
            ot_out.at[d - 1], ot_in.at[d - 1], o_s.at[d - 1], o_r.at[d - 1], device_id=back, device_id_type=MESH)
        cpo.start()
        o_copies += [cpm, cpo]
        pending += [cpm, cpo]
    nk_ref[...] = k_new
    nv_ref[...] = v_new
    m0, l0, ot0 = attend(0)
    for cp in o_copies:
        cp.wait_recv()
    top = m0
    for d in range(1, K):
        top = jnp.maximum(top, ml_in[d - 1, 0:1, :])
    f = jnp.exp(m0 - top)
    l_all = l0 * f
    o_all = ot0 * f
    for d in range(1, K):
        f = jnp.exp(ml_in[d - 1, 0:1, :] - top)
        l_all = l_all + ml_in[d - 1, 1:2, :] * f
        o_all = o_all + ot_in[d - 1].astype(jnp.float32) * f
    att_own[...] = (o_all / l_all).T.astype(jnp.bfloat16)

    att_copies = []
    for s in range(qb // c):
        first = z * qb + s * c
        tp_own = first // tok
        slot = lax.rem(tp_own - t + T, T)
        at = lax.rem(first, tok) // c
        for e in list(range(1, K)) + [0]:
            cp = pltpu.make_async_remote_copy(
                att_own.at[pl.ds(s * c, c)], att_in.at[slot, at], a_s.at[s, e], a_r.at[slot, at],
                device_id={"tp": tp_own, "kv": kv_peer(e)}, device_id_type=MESH)
            if e:
                cp.start()
                att_copies.append((cp, None))
            else:
                @pl.when(slot != 0)
                def _():
                    cp.start()

                @pl.when(slot == 0)
                def _():
                    att_in[0, at] = att_own[s * c:(s + 1) * c]

                att_copies.append((cp, slot))
    for cp in wo_copies:
        cp.wait_recv()
    for d in range(T):
        for i in range(tok // c):
            def wait_in():
                pltpu.make_async_remote_copy(
                    att_in.at[d, i], att_in.at[d, i], a_s.at[0, 0], a_r.at[d, i],
                    device_id={"kv": kv_peer(1)}, device_id_type=MESH).wait_recv()
            if d:
                wait_in()
            else:
                pl.when((t * tok + i * c) // qb != z)(wait_in)
    att = jnp.concatenate([att_in[d].reshape(tok, hd) for d in range(T)], axis=1)
    out_bias = row(outb_ref)
    wide = 256 if feat % 256 == 0 else feat
    for g in range(feat // wide):
        cols = slice(g * wide, (g + 1) * wide)
        w = jnp.concatenate([wout_v[d, :, cols] for d in range(T)], axis=0)
        y = jnp.dot(att, w, preferred_element_type=jnp.float32)
        y = y + out_bias[:, cols] + x_v[:, cols].astype(jnp.float32)
        out_ref[:, cols] = y.astype(jnp.bfloat16)

    for cp in pending:
        cp.wait_send()
    for cp, off in rs_copies:
        pl.when(off != 0)(cp.wait_send)
    for cp, slot in att_copies:
        if slot is None:
            cp.wait_send()
        else:
            pl.when(slot != 0)(cp.wait_send)


def place(a_ref, b_ref, c_ref, a_out, b_out, c_out, sem):
    copies = [
        pltpu.make_async_copy(src, dst, sem.at[i])
        for i, (src, dst) in enumerate(((a_ref, a_out), (b_ref, b_out), (c_ref, c_out)))
    ]
    for cp in copies:
        cp.start()
    for cp in copies:
        cp.wait()


def on_device(T, K, hidden_in, lengths, ln_gain, ln_bias, w_qkv, qkv_bias, cache_keys, cache_values, w_out, out_bias):
    _, tok, feat = hidden_in.shape
    hd = cache_keys.shape[3]
    part_len = cache_keys.shape[2]
    group = T * tok
    qb = group // K
    c = min(tok, qb)
    tokp = max(tok, LANES)
    bf, f32 = jnp.bfloat16, jnp.float32
    dma = pltpu.SemaphoreType.DMA
    any_spec = pl.BlockSpec(memory_space=pltpu.HBM)
    vm = pl.BlockSpec(memory_space=pltpu.VMEM)
    n1 = max(T - 1, 1)
    out, nk, nv = pl.pallas_call(
        functools.partial(kernel, T, K, feat * K),
        out_shape=(
            jax.ShapeDtypeStruct((tok, feat), bf),
            jax.ShapeDtypeStruct((qb, hd), bf),
            jax.ShapeDtypeStruct((qb, hd), bf),
        ),
        in_specs=[pl.BlockSpec(memory_space=pltpu.SMEM)] + [any_spec] * 5 + [vm] * 4,
        out_specs=(vm, vm, vm),
        scratch_shapes=[
            pltpu.VMEM((tok, feat), bf),
            pltpu.VMEM((feat, 3 * hd), bf),
            pltpu.VMEM((part_len, hd), bf),
            pltpu.VMEM((part_len, hd), bf),
            pltpu.VMEM((T, hd, feat), bf),
            pltpu.VMEM((8, tokp), f32),
            pltpu.VMEM((K - 1, 8, tokp), f32),
            pltpu.VMEM((T, tok, feat), bf),
            pltpu.VMEM((T, tok, hd), f32),
            pltpu.VMEM((T, tok, 2 * hd), f32),
            pltpu.VMEM((K, qb // c, c, hd), f32),
            pltpu.VMEM((K, qb // c, c, 2 * hd), f32),
            pltpu.VMEM((K, qb, hd), bf),
            pltpu.VMEM((K - 1, hd, qb), bf),
            pltpu.VMEM((K - 1, hd, qb), bf),
            pltpu.VMEM((K - 1, 8, qb), f32),
            pltpu.VMEM((K - 1, 8, qb), f32),
            pltpu.VMEM((qb, hd), bf),
            pltpu.VMEM((T, tok // c, c, hd), bf),
            dma((5,)),
            dma((K - 1,)), dma((K - 1,)),
            dma((n1,)), dma((n1,)),
            dma((n1,)), dma((n1,)),
            dma((T * (tok // c),)), dma((K - 1, qb // c)),
            dma((T * (tok // c),)), dma((K - 1, qb // c)),
            dma((K - 1,)), dma((K - 1,)),
            dma((K - 1,)), dma((K - 1,)),
            dma((K - 1,)), dma((K - 1,)),
            dma((qb // c, K)), dma((T, tok // c)),
        ],
        compiler_params=pltpu.CompilerParams(
            collective_id=0, has_side_effects=True),
    )(lengths, hidden_in[0], w_qkv, cache_keys[0, 0], cache_values[0, 0], w_out, ln_gain, ln_bias, out_bias, qkv_bias)
    held = [pl.BlockSpec(memory_space=pl.ANY)] * 3
    out, nk, nv = pl.pallas_call(
        place,
        out_shape=tuple(jax.ShapeDtypeStruct(a.shape, a.dtype) for a in (out, nk, nv)),
        in_specs=held,
        out_specs=tuple(held),
        scratch_shapes=[dma((3,))],
    )(out, nk, nv)
    return out[None], nk[None, None], nv[None, None]


def solution(mesh):
    placed = (
        P("req", "tp", "kv"),
        P("req"),
        P("kv"),
        P("kv"),
        P("kv", "tp"),
        P("tp"),
        P("req", "tp", "kv", None),
        P("req", "tp", "kv", None),
        P("tp", "kv"),
        P("kv"),
    )
    return jax.shard_map(
        functools.partial(on_device, mesh.shape["tp"], mesh.shape["kv"]),
        mesh=mesh,
        in_specs=placed,
        out_specs=(P("req", "tp", "kv"), P("req", "tp", "kv", None), P("req", "tp", "kv", None)),
        check_vma=False,
    )
```
